32 devices in a mesh: blk: 8 (over y, x, core), tm: 4 (over z).
Axes of the slice: x: 2, y: 2, z: 4, core: 2. Of those that a mesh axis runs over, the one named last changes fastest.
Arguments:
- occupied_orbitals: float32 [2048, 1024], P(None, 'blk'), may hold values from -0.6 to 0.6
- empty_orbitals: float32 [2048, 1024], P(None, 'blk'), may hold values from -0.6 to 0.6
- occupied_energy: float32 [2048], replicated, may hold values from -1.5 to -0.05
- empty_energy: float32 [2048], replicated, may hold values from 0.05 to 1.5
- time_points: float32 [4], replicated, may hold values from 0.25 to 4
- pair_table: int32 [4], replicated, may hold values from 0 to 3, each once
Outputs:
- polarizability: float32 [4, 2, 1024, 512], P('tm', None, 'blk')
The draws below stay inside these ranges and needn't reach their ends.
Inputs may be any that keep to these rules, and one draw needn't show every extreme that they name: `pair_table`: each of 0 to 3 appears exactly once.
All inputs are finite; a program needn't handle non-finite values.
Results may differ from the reference program's by a relative error of at most 0.000088.
Values sent between devices are 32-bit elements; how exact they have to be, the bound alone decides.
No kernel may reach another device: no remote copies, remote signals or barrier semaphores. Data moves between devices by JAX's collectives and lax.ppermute only.
A program may use at most 64 MiB of HBM per device.

```python
import math
import jax
import jax.numpy as jnp
from jax import lax

NST = 2048
TAU_DEV = 2
R = 1024
NPAIR = 4
N_TM = 4


def levels(stream_key, extent, cuts, smallest, top_value):
    level, own = 1.0, jax.random.fold_in(stream_key, 6)
    for axis_at, parts in cuts:
        draws = jnp.exp(jax.random.uniform(jax.random.fold_in(own, axis_at), (parts,), jnp.float32, smallest / len(cuts), top_value / len(cuts)))
        level = level * jnp.repeat(draws, extent[axis_at] // parts).reshape([-1 if axis == axis_at else 1 for axis in range(len(extent))])
    return level


def centred(stream_key, shape, spread, limit, pieces=(), kind=jnp.bfloat16):
    loudness = levels(stream_key, shape, pieces, -0.22, 0.18) if pieces else 1.0
    result = jax.random.normal(stream_key, shape, jnp.float32) * spread * loudness
    return jnp.minimum(jnp.maximum(result, -limit), limit).astype(kind)


def setup_inputs(seed: int = 0) -> dict:
    streams_of = jax.random.split(jax.random.key(seed), 7)
    occupied_orbitals = centred(streams_of[0], (NST, R), 0.1, 0.6, ((1, 8),), jnp.float32)
    empty_orbitals = centred(streams_of[1], (NST, R), 0.1, 0.6, ((1, 8),), jnp.float32)
    occupied_energy = jnp.clip(jax.random.uniform(streams_of[2], (NST,), jnp.float32, -1.5, -0.05), -1.5, -0.05)
    empty_energy = jnp.clip(jax.random.uniform(streams_of[3], (NST,), jnp.float32, 0.05, 1.5), 0.05, 1.5)
    time_points = jnp.clip(jnp.exp(jax.random.uniform(streams_of[4], (NPAIR,), jnp.float32, math.log(0.25), math.log(4.0))), 0.25, 4.0)
    pair_table = jax.random.permutation(streams_of[5], NPAIR).astype(jnp.int32)
    return dict(occupied_orbitals=occupied_orbitals, empty_orbitals=empty_orbitals, occupied_energy=occupied_energy, empty_energy=empty_energy, time_points=time_points, pair_table=pair_table)


def reference(occupied_orbitals, empty_orbitals, occupied_energy, empty_energy, time_points, pair_table):
    chosen = time_points[pair_table]

    def slot_field(moment):
        empty_weight = jnp.exp(-empty_energy * moment)
        occupied_weight = jnp.exp(occupied_energy * moment)
        empty_green = jnp.dot((empty_orbitals * empty_weight[:, None]).T, empty_orbitals,
                              precision=lax.Precision.HIGHEST, preferred_element_type=jnp.float32)
        occupied_green = jnp.dot((occupied_orbitals * occupied_weight[:, None]).T, occupied_orbitals,
                                 precision=lax.Precision.HIGHEST, preferred_element_type=jnp.float32)
        return -(empty_green * occupied_green)

    fields = lax.map(slot_field, chosen)
    fields = fields.reshape(N_TM // 2, TAU_DEV, R, 2, R // 2)
    fields = jnp.transpose(fields, (0, 3, 1, 2, 4))
    return fields.reshape(N_TM, TAU_DEV, R, R // 2)
```

```python
import functools

import jax
import jax.numpy as jnp
from jax import lax
from jax.experimental import pallas as pl
from jax.experimental.pallas import tpu as pltpu
from jax.sharding import PartitionSpec as P

AXES = ("blk", "tm")
TAU_DEV = 2
STEP = 256
SHARES = (5, 3)

VMEM = pl.BlockSpec(memory_space=pltpu.VMEM)
SMEM = pl.BlockSpec(memory_space=pltpu.SMEM)
ANY = pl.BlockSpec(memory_space=pl.ANY)
F32, BF16 = jnp.float32, jnp.bfloat16


def moved(value, target):
    rows, columns = lax.axis_size("blk"), lax.axis_size("tm")
    pairs = []
    for row in range(rows):
        for column in range(columns):
            chip, core, pair, half = target(row // 2, row % 2, column // 2, column % 2)
            pairs.append((row * columns + column, (chip * 2 + core) * columns + pair * 2 + half))
    return lax.ppermute(value, AXES, pairs)


def place():
    row, column = lax.axis_index("blk"), lax.axis_index("tm")
    return row >> 1, row & 1, column >> 1, column & 1


def bit_of(chip, step):
    return (chip >> ((step & -step).bit_length() - 1)) & 1


def near(value):
    return pltpu.with_memory_space_constraint(value, pltpu.VMEM)


def call(kernel, shapes, specs, *args, cost=None, **more):
    flops, moved_bytes = cost or (0, 0)
    return pl.pallas_call(
        kernel,
        out_shape=shapes,
        in_specs=specs,
        compiler_params=pltpu.CompilerParams(vmem_limit_bytes=16 << 20),
        cost_estimate=pl.CostEstimate(flops=flops, bytes_accessed=moved_bytes, transcendentals=0),
        **more,
    )(*(near(arg) if spec is VMEM else arg for arg, spec in zip(args, specs)))


def turned(value):
    return pltpu.roll(value, value.shape[-1] // 2, value.ndim - 1)


def front(shape):
    return lax.broadcasted_iota(jnp.int32, shape, len(shape) - 1) < shape[-1] // 2


def parts(value):
    high = value.astype(BF16)
    return high, (value - high.astype(F32)).astype(BF16)


def product(left, right):
    left_high, left_low = left
    right_high, right_low = right
    dot = functools.partial(jnp.dot, preferred_element_type=F32)
    return dot(left_high, right_high) + (dot(left_low, right_high) + dot(left_high, right_low))


def pack_kernel(empty, occupied, *out, steps):
    chip, core, _, half = place()
    e, o = empty[...], occupied[...]
    first = front(e.shape)
    rows = pl.ds(pl.program_id(0) * e.shape[0], e.shape[0])
    for index, step in enumerate(steps):
        top = index == len(steps) - 1
        low = (
            (half if top else half ^ 1 ^ bit_of(chip, step)) == 0
        )
        e_first = core == (1 if top else 0)
        a, b = jnp.where(e_first, e, o), jnp.where(e_first, o, e)
        straight, other = jnp.where(low, a, b), turned(jnp.where(low, b, a))
        out[index][rows, :] = jnp.where(first == low, straight, other)


def own_kernel(pair_table, time_points, e_energy, o_energy, e, o, e_twin, o_twin, weights, tile, *flat):
    _, core, pair, _ = place()
    states, width = e.shape
    for slot in range(TAU_DEV):
        moment = time_points[pair_table[pair * TAU_DEV + slot]]
        weights[slot : slot + 1, :] = jnp.exp(-e_energy[...] * moment)
        weights[TAU_DEV + slot : TAU_DEV + slot + 1, :] = jnp.exp(o_energy[...] * moment)
    sums = []
    for kind, (mine, twin) in enumerate(((e, e_twin), (o, o_twin))):
        total = 0.0
        for at in range(0, states, STEP):
            here, other = mine[at : at + STEP, :], twin[at : at + STEP, :]
            flipped = here.T
            left = jnp.concatenate(
                [flipped * weights[kind * TAU_DEV + slot, at : at + STEP][None, :] for slot in range(TAU_DEV)], axis=0
            )
            left = parts(left)
            flat[2 * kind][:, at : at + STEP] = left[0]
            flat[2 * kind + 1][:, at : at + STEP] = left[1]
            right = jnp.concatenate([jnp.where(core == 0, here, other), jnp.where(core == 0, other, here)], axis=1)
            total = total + product(left, parts(right))
        sums.append(total)
    tile[...] = -(sums[0] * sums[1]).reshape(tile.shape)


def green_kernel(weights, *rest, start, last):
    flat, (x_own, y_own, x_twin, y_twin), rest = rest[:4], rest[4:8], rest[8:]
    chip, core, _, half_index = place()
    width = x_own.shape[1]
    rows = TAU_DEV * width
    totals = [0.0, 0.0]
    mask = front((STEP, width)) == (core == 0)
    for at in range(0, x_own.shape[0], STEP):
        xo, yo = x_own[at : at + STEP, :], y_own[at : at + STEP, :]
        xt, yt = x_twin[at : at + STEP, :], y_twin[at : at + STEP, :]
        states = slice(start + at, start + at + STEP)
        for kind, mid, x, y in (
            (0, jnp.where(mask, xo, yo), jnp.where(mask, xo, xt), jnp.where(mask, yt, yo)),
            (1, jnp.where(mask, yo, xo), jnp.where(mask, xt, xo), jnp.where(mask, yo, yt)),
        ):
            flipped = mid.T
            left = parts(
                jnp.concatenate(
                    [flipped * weights[kind * TAU_DEV + slot, states][None, :] for slot in range(TAU_DEV)], axis=0
                )
            )
            left = [
                jnp.concatenate([flat[2 * kind + part][:, states], left[part]], axis=0) for part in range(2)
            ]
            totals[kind] = totals[kind] + product(left, parts(jnp.concatenate([x, y], axis=1)))
    if not last:
        rest[0][...] = totals[0]
        rest[1][...] = totals[1]
        return
    before, (to_x, to_y, to_half, kept) = rest[:-4], rest[-4:]
    e, o = totals
    if before:
        e, o = e + before[0][...], o + before[1][...]
    o = jnp.concatenate([turned(o[:, :width]), turned(o[:, width:])], axis=1)
    same = (chip // (lax.axis_size("blk") // 4)) == half_index
    cut = width // 2
    for slot in range(TAU_DEV):
        g, q = e[slot * width : (slot + 1) * width, :], o[slot * width : (slot + 1) * width, :]
        x, y = -(g[:, :width] * q[:, :width]), turned(-(g[:, width:] * q[:, width:]))
        kept[slot] = jnp.where(same, x, y)
        to_half[slot] = jnp.where(same, y, x)
        at = rows + slot * width
        g, q = e[at : at + width, :], o[at : at + width, :]
        a, b = -(g[:cut] * q[cut:]), -(g[cut:] * q[:cut])
        to_x[slot] = turned(jnp.where(core == 0, a, b)[:, width:])
        to_y[slot] = jnp.where(core == 0, b, a)[:, :width]


def joined(low, high):
    first = front(low.shape)
    return jnp.concatenate([jnp.where(first, low, turned(high)), jnp.where(first, turned(low), high)], axis=1)


def edge_kernel(tile, *rest, steps):
    pieces, out = rest[:-1], rest[-1]
    chip, _, _, half = place()
    chips = steps[-1]
    same, width = (chip // chips) == half, tile.shape[-1]
    slot = pl.program_id(0)
    position = chip & (chips - 1)

    def columns(at):
        return pl.ds(pl.multiple_of(at * width, width), width)

    for index, step in enumerate(steps[:-1]):
        kept, came = pieces[2 * index][slot], pieces[2 * index + 1][slot]
        held = jnp.where(same, half ^ bit_of(chip, step), half) == 0
        edge = joined(jnp.where(held, kept, came), jnp.where(held, came, kept))
        if index == 0:
            out[0, 0, :, columns(position)] = jnp.where(same, tile[slot], edge)
        out[0, 0, :, columns(position ^ step)] = edge


def corner_kernel(*rest, steps):
    pieces, (out, built, semaphore) = rest[:-4], rest[-3:]
    chip, _, _, half = place()
    chips = steps[-1]
    position = chip & (chips - 1)
    width = built.shape[-1]

    @pl.when((chip // chips) != half)
    def _():
        copies = []
        for index, step in enumerate(steps[:-1]):
            x_here, y_here, x_far, y_far = pieces[4 * index : 4 * index + 4]
            straight = bit_of(chip, step) == 0
            for slot in range(TAU_DEV):
                x = jnp.where(half == 0, x_here[slot], x_far[slot]), jnp.where(half == 0, x_far[slot], x_here[slot])
                y = jnp.where(half == 0, y_here[slot], y_far[slot]), jnp.where(half == 0, y_far[slot], y_here[slot])
                top = joined(jnp.where(straight, y[0], x[0]), jnp.where(straight, x[1], y[0]))
                low = joined(jnp.where(straight, x[0], y[1]), jnp.where(straight, y[1], x[1]))
                built[index, slot] = jnp.concatenate([top, low], axis=0)
            at = pl.multiple_of((position ^ step) * width, width)
            copies.append(
                pltpu.make_async_copy(built.at[index], out.at[0, :, :, pl.ds(at, width)], semaphore.at[index])
            )
            copies[-1].start()
        for copy in copies:
            copy.wait()


def body(occupied, empty, o_energy, e_energy, time_points, pair_table):
    states, width = occupied.shape
    top = lax.axis_size("blk") // 4
    steps = tuple(range(1, top)) + (top,)
    cuts = [states * sum(SHARES[:index]) // sum(SHARES) // STEP * STEP for index in range(len(SHARES) + 1)]

    def tile_at(rows):
        return pltpu.VMEM((TAU_DEV, rows, width), F32)

    crossed = []
    for start, stop in zip(cuts, cuts[1:]):
        block = pl.BlockSpec((STEP, width), lambda at, first=start // STEP: (first + at, 0))
        packed = call(
            functools.partial(pack_kernel, steps=steps),
            [pltpu.VMEM((stop - start, width), F32)] * len(steps),
            [block, block],
            empty,
            occupied,
            out_specs=[VMEM] * len(steps),
            grid=((stop - start) // STEP,),
            cost=(0, 4 * (stop - start) * width * 4),
        )
        crossed.append([
            moved(value, lambda v, c, p, h, step=step: (v ^ step, c, p, h)) for value, step in zip(packed, steps)
        ])

    def twin(value):
        return moved(value, lambda v, c, p, h: (v, 1 - c, p, h))

    weights, tile, *flat = call(
        own_kernel,
        [pltpu.VMEM((2 * TAU_DEV, states), F32), pltpu.VMEM((TAU_DEV, width, 2 * width), F32)]
        + [pltpu.VMEM((TAU_DEV * width, states), BF16)] * 4,
        [SMEM] * 2 + [VMEM] * 6,
        pair_table, time_points, e_energy[None], o_energy[None], empty, occupied, twin(empty), twin(occupied),
        out_specs=[VMEM] * 6,
        cost=(3 * 4 * 2 * states * width * width * 4, 4 * states * width * 4),
    )
    both = [[(value, twin(value)) for value in values] for values in crossed]
    edges, corners = [], []
    for index, step in enumerate(steps[:-1]):
        sums = ()
        for start, stop, values in zip(cuts, cuts[1:], both):
            last = stop == states
            (x_own, x_twin), (y_own, y_twin) = values[index], values[-1]
            shapes = [pltpu.VMEM((2 * TAU_DEV * width, 2 * width), F32)] * 2
            if last:
                shapes = [tile_at(width // 2)] * 2 + [tile_at(width)] * 2
            sums = call(
                functools.partial(green_kernel, start=start, last=last),
                shapes,
                [VMEM] * (9 + len(sums)),
                weights, *flat, x_own, y_own, x_twin, y_twin, *sums,
                out_specs=[VMEM] * len(shapes),
                cost=(3 * 2 * 2 * (stop - start) * 4 * width * 2 * width, 0),
            )
        to_x, to_y, to_half, kept = sums

        def other_half(value):
            return moved(value, lambda v, c, p, h: (v, c, p, 1 - h))

        from_x = moved(to_x, lambda v, c, p, h, step=step: (v ^ step, c, p, h))
        from_y = moved(to_y, lambda v, c, p, h: (v ^ top, c, p, h))
        edges += [kept, other_half(to_half)]
        corners += [from_x, from_y, other_half(from_x), other_half(from_y)]
    shape = (1, TAU_DEV, width, 2 * width * top)
    out = call(
        functools.partial(edge_kernel, steps=steps),
        jax.ShapeDtypeStruct(shape, F32),
        [VMEM] * (1 + len(edges)),
        tile, *edges,
        out_specs=pl.BlockSpec((1, 1) + shape[2:], lambda slot: (0, slot, 0, 0)),
        grid=(TAU_DEV,),
        cost=(0, 4 * TAU_DEV * width * 2 * width * top),
    )
    return call(
        functools.partial(corner_kernel, steps=steps),
        jax.ShapeDtypeStruct(shape, F32),
        [VMEM] * len(corners) + [ANY],
        *corners, out,
        out_specs=ANY,
        scratch_shapes=[
            pltpu.VMEM((len(steps) - 1, TAU_DEV, width, 2 * width), F32), pltpu.SemaphoreType.DMA((len(steps) - 1,))
        ],
        input_output_aliases={len(corners): 0},
    )


def solution(mesh):
    return jax.shard_map(
        body,
        mesh=mesh,
        in_specs=(P(None, "blk"), P(None, "blk"), P(), P(), P(), P()),
        out_specs=P("tm", None, "blk", None),
        check_vma=False,
    )
```

```python
import functools

import jax
import jax.numpy as jnp
from jax import lax
from jax.experimental import pallas as pl
from jax.experimental.pallas import tpu as pltpu
from jax.sharding import PartitionSpec as P


AXES = ("blk", "tm")
TAU_DEV = 2
STEP = 256
SHARES = (2, 4, 2)

FAR = pl.BlockSpec(memory_space=pltpu.HBM)
VMEM = pl.BlockSpec(memory_space=pltpu.VMEM)
SMEM = pl.BlockSpec(memory_space=pltpu.SMEM)
ANY = pl.BlockSpec(memory_space=pl.ANY)
F32, BF16 = jnp.float32, jnp.bfloat16


def moved(value, target):
    rows, columns = lax.axis_size("blk"), lax.axis_size("tm")
    pairs = []
    for row in range(rows):
        for column in range(columns):
            chip, core, pair, half = target(row // 2, row % 2, column // 2, column % 2)
            pairs.append((row * columns + column, (chip * 2 + core) * columns + pair * 2 + half))
    return lax.ppermute(value, AXES, pairs)


def place():
    row, column = lax.axis_index("blk"), lax.axis_index("tm")
    return row >> 1, row & 1, column >> 1, column & 1


def bit_of(chip, step):
    return (chip >> ((step & -step).bit_length() - 1)) & 1


def near(value):
    return pltpu.with_memory_space_constraint(value, pltpu.VMEM)


def call(kernel, shapes, specs, *args, cost=None, **more):
    flops, moved_bytes = cost or (0, 0)
    return pl.pallas_call(
        kernel,
        out_shape=shapes,
        in_specs=specs,
        compiler_params=pltpu.CompilerParams(vmem_limit_bytes=16 << 20),
        cost_estimate=pl.CostEstimate(flops=flops, bytes_accessed=moved_bytes, transcendentals=0),
        **more,
    )(*(near(arg) if spec is VMEM else arg for arg, spec in zip(args, specs)))


def turned(value):
    return pltpu.roll(value, value.shape[-1] // 2, value.ndim - 1)


def front(shape):
    return lax.broadcasted_iota(jnp.int32, shape, len(shape) - 1) < shape[-1] // 2


def parts(value):
    high = value.astype(BF16)
    return high, (value - high.astype(F32)).astype(BF16)


def product(left, right):
    left_high, left_low = left
    right_high, right_low = right
    dot = functools.partial(jnp.dot, preferred_element_type=F32)
    return dot(left_high, right_high) + (dot(left_low, right_high) + dot(left_high, right_low))


def pack_kernel(empty, occupied, *rest, steps, start):
    out, (held, semaphores) = rest[:-2], rest[-2:]
    chip, core, _, half = place()
    rows, width = held.shape[1:]
    copies = [
        [
            pltpu.make_async_copy(
                source.at[pl.ds(start + at, STEP), :], held.at[kind, pl.ds(at, STEP), :], semaphores.at[kind, at // STEP]
            )
            for kind, source in enumerate((empty, occupied))
        ]
        for at in range(0, rows, STEP)
    ]
    for pair in copies:
        for copy in pair:
            copy.start()
    first = front((STEP, width))
    for at, pair in zip(range(0, rows, STEP), copies):
        for copy in pair:
            copy.wait()
        e, o = held[0, at : at + STEP, :], held[1, at : at + STEP, :]
        for index, step in enumerate(steps):
            top = index == len(steps) - 1
            low = (half if top else half ^ 1 ^ bit_of(chip, step)) == 0
            e_first = core == (1 if top else 0)
            a, b = jnp.where(e_first, e, o), jnp.where(e_first, o, e)
            straight, other = jnp.where(low, a, b), turned(jnp.where(low, b, a))
            out[index][at : at + STEP, :] = jnp.where(first == low, straight, other)


def own_kernel(pair_table, time_points, e_energy, o_energy, e, o, e_twin, o_twin, weights, tile, *flat):
    _, core, pair, _ = place()
    states, _ = e.shape
    for slot in range(TAU_DEV):
        moment = time_points[pair_table[pair * TAU_DEV + slot]]
        weights[slot : slot + 1, :] = jnp.exp(-e_energy[...] * moment)
        weights[TAU_DEV + slot : TAU_DEV + slot + 1, :] = jnp.exp(o_energy[...] * moment)
    sums = []
    for kind, (mine, twin) in enumerate(((e, e_twin), (o, o_twin))):
        total = 0.0
        for at in range(0, states, STEP):
            here, other = mine[at : at + STEP, :], twin[at : at + STEP, :]
            flipped = here.T
            left = jnp.concatenate(
                [flipped * weights[kind * TAU_DEV + slot, at : at + STEP][None, :] for slot in range(TAU_DEV)], axis=0
            )
            left = parts(left)
            flat[2 * kind][:, at : at + STEP] = left[0]
            flat[2 * kind + 1][:, at : at + STEP] = left[1]
            right = jnp.concatenate([jnp.where(core == 0, here, other), jnp.where(core == 0, other, here)], axis=1)
            total = total + product(left, parts(right))
        sums.append(total)
    tile[...] = -(sums[0] * sums[1]).reshape(tile.shape)


def green_kernel(weights, *rest, start, last):
    flat, (x_own, y_own, x_twin, y_twin), rest = rest[:4], rest[4:8], rest[8:]
    chip, core, _, half_index = place()
    width = x_own.shape[1]
    rows = TAU_DEV * width
    totals = [0.0, 0.0]
    mask = front((STEP, width)) == (core == 0)
    for at in range(0, x_own.shape[0], STEP):
        xo, yo = x_own[at : at + STEP, :], y_own[at : at + STEP, :]
        xt, yt = x_twin[at : at + STEP, :], y_twin[at : at + STEP, :]
        states = slice(start + at, start + at + STEP)
        for kind, mid, x, y in (
            (0, jnp.where(mask, xo, yo), jnp.where(mask, xo, xt), jnp.where(mask, yt, yo)),
            (1, jnp.where(mask, yo, xo), jnp.where(mask, xt, xo), jnp.where(mask, yo, yt)),
        ):
            flipped = mid.T
            left = parts(
                jnp.concatenate(
                    [flipped * weights[kind * TAU_DEV + slot, states][None, :] for slot in range(TAU_DEV)], axis=0
                )
            )
            left = [
                jnp.concatenate([flat[2 * kind + part][:, states], left[part]], axis=0) for part in range(2)
            ]
            totals[kind] = totals[kind] + product(left, parts(jnp.concatenate([x, y], axis=1)))
    out = 4 if last else 2
    before, rest = rest[:-out], rest[-out:]
    for kind, value in enumerate(before):
        totals[kind] = totals[kind] + value[...]
    e, o = totals
    if not last:
        rest[0][...], rest[1][...] = e, o
        return
    to_x, to_y, to_half, kept = rest
    o = jnp.concatenate([turned(o[:, :width]), turned(o[:, width:])], axis=1)
    same = (chip // (lax.axis_size("blk") // 4)) == half_index
    cut = width // 2
    for slot in range(TAU_DEV):
        g, q = e[slot * width : (slot + 1) * width, :], o[slot * width : (slot + 1) * width, :]
        x, y = -(g[:, :width] * q[:, :width]), turned(-(g[:, width:] * q[:, width:]))
        kept[slot] = jnp.where(same, x, y)
        to_half[slot] = jnp.where(same, y, x)
        at = rows + slot * width
        g, q = e[at : at + width, :], o[at : at + width, :]
        a, b = -(g[:cut] * q[cut:]), -(g[cut:] * q[:cut])
        to_x[slot] = turned(jnp.where(core == 0, a, b)[:, width:])
        to_y[slot] = jnp.where(core == 0, b, a)[:, :width]


def joined(low, high):
    first = front(low.shape)
    return jnp.concatenate([jnp.where(first, low, turned(high)), jnp.where(first, turned(low), high)], axis=1)


def edge_kernel(tile, *rest, steps):
    pieces, out = rest[:-1], rest[-1]
    chip, _, _, half = place()
    chips = steps[-1]
    same, width = (chip // chips) == half, tile.shape[-1]
    slot = pl.program_id(0)
    position = chip & (chips - 1)

    def columns(at):
        return pl.ds(pl.multiple_of(at * width, width), width)

    for index, step in enumerate(steps[:-1]):
        kept, came = pieces[2 * index][slot], pieces[2 * index + 1][slot]
        held = jnp.where(same, half ^ bit_of(chip, step), half) == 0
        edge = joined(jnp.where(held, kept, came), jnp.where(held, came, kept))
        if index == 0:
            out[0, 0, :, columns(position)] = jnp.where(same, tile[slot], edge)
        out[0, 0, :, columns(position ^ step)] = edge


def corner_kernel(*rest, steps):
    pieces, (out, built, semaphore) = rest[:-4], rest[-3:]
    chip, _, _, half = place()
    chips = steps[-1]
    position = chip & (chips - 1)
    width = built.shape[-1]

    @pl.when((chip // chips) != half)
    def _():
        copies = []
        for index, step in enumerate(steps[:-1]):
            x_here, y_here, x_far, y_far = pieces[4 * index : 4 * index + 4]
            straight = bit_of(chip, step) == 0
            for slot in range(TAU_DEV):
                x = jnp.where(half == 0, x_here[slot], x_far[slot]), jnp.where(half == 0, x_far[slot], x_here[slot])
                y = jnp.where(half == 0, y_here[slot], y_far[slot]), jnp.where(half == 0, y_far[slot], y_here[slot])
                top = joined(jnp.where(straight, y[0], x[0]), jnp.where(straight, x[1], y[0]))
                low = joined(jnp.where(straight, x[0], y[1]), jnp.where(straight, y[1], x[1]))
                built[index, slot] = jnp.concatenate([top, low], axis=0)
            at = pl.multiple_of((position ^ step) * width, width)
            copies.append(
                pltpu.make_async_copy(built.at[index], out.at[0, :, :, pl.ds(at, width)], semaphore.at[index])
            )
            copies[-1].start()
        for copy in copies:
            copy.wait()


def body(occupied, empty, o_energy, e_energy, time_points, pair_table):
    states, width = occupied.shape
    top = lax.axis_size("blk") // 4
    steps = tuple(range(1, top)) + (top,)
    cuts = [states * sum(SHARES[:index]) // sum(SHARES) // STEP * STEP for index in range(len(SHARES) + 1)]

    def tile_at(rows):
        return pltpu.VMEM((TAU_DEV, rows, width), F32)

    crossed = []
    for part, (start, stop) in enumerate(zip(cuts, cuts[1:])):
        packed = call(
            functools.partial(pack_kernel, steps=steps, start=start),
            [pltpu.VMEM((stop - start, width), F32)] * len(steps),
            [FAR, FAR],
            pltpu.with_memory_space_constraint(empty, pltpu.HBM),
            pltpu.with_memory_space_constraint(occupied, pltpu.HBM),
            out_specs=[VMEM] * len(steps),
            scratch_shapes=[
                pltpu.VMEM((2, stop - start, width), F32), pltpu.SemaphoreType.DMA((2, (stop - start) // STEP))
            ],
            cost=(0, 4 * (stop - start) * width * 4),
        )
        if not part:
            *packed, own_e, own_o = lax.optimization_barrier((*packed, empty, occupied))
        crossed.append([
            moved(value, lambda v, c, p, h, step=step: (v ^ step, c, p, h)) for value, step in zip(packed, steps)
        ])

    def twin(value):
        return moved(value, lambda v, c, p, h: (v, 1 - c, p, h))

    twins = twin(own_e), twin(own_o)
    weights, tile, *flat = call(
        own_kernel,
        [pltpu.VMEM((2 * TAU_DEV, states), F32), pltpu.VMEM((TAU_DEV, width, 2 * width), F32)]
        + [pltpu.VMEM((TAU_DEV * width, states), BF16)] * 4,
        [SMEM] * 2 + [VMEM] * 6,
        pair_table, time_points, e_energy[None], o_energy[None], own_e, own_o, *twins,
        out_specs=[VMEM] * 6,
        cost=(3 * 4 * 2 * states * width * width * 4, 4 * states * width * 4),
    )
    both = []
    for values in crossed:
        both.append([(value, twin(value)) for value in values])
    edges, corners = [], []
    for index, step in enumerate(steps[:-1]):
        sums = ()
        for start, stop, values in zip(cuts, cuts[1:], both):
            last = stop == states
            (x_own, x_twin), (y_own, y_twin) = values[index], values[-1]
            shapes = [pltpu.VMEM((2 * TAU_DEV * width, 2 * width), F32)] * 2
            if last:
                shapes = [tile_at(width // 2)] * 2 + [tile_at(width)] * 2
            sums = call(
                functools.partial(green_kernel, start=start, last=last),
                shapes,
                [VMEM] * (9 + len(sums)),
                weights, *flat, x_own, y_own, x_twin, y_twin, *sums,
                out_specs=[VMEM] * len(shapes),
                cost=(3 * 2 * 2 * (stop - start) * 4 * width * 2 * width, 0),
            )
        to_x, to_y, to_half, kept = sums

        def other_half(value):
            return moved(value, lambda v, c, p, h: (v, c, p, 1 - h))

        from_x = moved(to_x, lambda v, c, p, h, step=step: (v ^ step, c, p, h))
        from_y = moved(to_y, lambda v, c, p, h: (v ^ top, c, p, h))
        edges += [kept, other_half(to_half)]
        corners += [from_x, from_y, other_half(from_x), other_half(from_y)]
    shape = (1, TAU_DEV, width, 2 * width * top)
    out = call(
        functools.partial(edge_kernel, steps=steps),
        jax.ShapeDtypeStruct(shape, F32),
        [VMEM] * (1 + len(edges)),
        tile, *edges,
        out_specs=pl.BlockSpec((1, 1) + shape[2:], lambda slot: (0, slot, 0, 0)),
        grid=(TAU_DEV,),
        cost=(0, 4 * TAU_DEV * width * 2 * width * top),
    )
    return call(
        functools.partial(corner_kernel, steps=steps),
        jax.ShapeDtypeStruct(shape, F32),
        [VMEM] * len(corners) + [ANY],
        *corners, out,
        out_specs=ANY,
        scratch_shapes=[
            pltpu.VMEM((len(steps) - 1, TAU_DEV, width, 2 * width), F32), pltpu.SemaphoreType.DMA((len(steps) - 1,))
        ],
        input_output_aliases={len(corners): 0},
    )


def solution(mesh):
    return jax.shard_map(
        body,
        mesh=mesh,
        in_specs=(P(None, "blk"), P(None, "blk"), P(), P(), P(), P()),
        out_specs=P("tm", None, "blk", None),
        check_vma=False,
    )
```
